256 devices in a mesh: section: 4 (over z_hi, core), kv: 16 (over z_lo, y), tp: 4 (over x).
Axes of the slice: x: 4, y: 4, z: 8 (z_hi: 2, z_lo: 4; z = z_hi * 4 + z_lo), core: 2. Of those that a mesh axis runs over, the one named last changes fastest.
Arguments:
- patches: bfloat16 [32768, 1152], P(('section', 'kv'), 'tp'), may hold values from -6 to 6
- vis_gain: float32 [1152], replicated, may hold values from 0.1 to 1.9
- vis_bias: float32 [1152], replicated, may hold values from -3 to 3
- w_proj: bfloat16 [1152, 4608], P('section', 'tp')
- b_proj: float32 [4608], P('tp'), may hold values from -12 to 12
- rms_gain: float32 [4608], P('tp'), may hold values from 0.1 to 1.9
- w_kv: bfloat16 [4608, 2, 1024], P('tp'), may hold values from -0.09375 to 0.09375
- queries: bfloat16 [16, 2048], P('section', 'tp'), may hold values from -18 to 18
- cache: bfloat16 [1024, 128, 2, 1024], P(('section', 'kv'), None, None, 'tp'), may hold values from -6 to 6
- cache_lengths: int32 [4, 4], P('section'), may hold values from 1 to 31872, 32256 in all within a row
- slot_page: int32 [4, 256], P('section', 'kv'), may hold values from 0 to 255, each once within a row
- page_owner: int32 [4, 64], replicated, may hold values from 0 to 15, as said below
- image_request: int32 [4, 2], P('section'), may hold values from 0 to 3
Outputs:
- new_pages: bfloat16 [2048, 128, 2, 1024], P(('section', 'kv'), None, None, 'tp')
- attended: bfloat16 [16, 2048], P('section', 'tp')
The draws below stay inside these ranges and needn't reach their ends.
Inputs may be any that keep to these rules, and one draw needn't show every extreme that they name: `page_owner`: from each source's 4 pages at most 2 go to any one owner; in every group one owner receives exactly 2 pages from every source.
All inputs are finite; a program needn't handle non-finite values.
Results may differ from the reference program's by a relative error of at most 0.0063.
Values may be sent and summed in bfloat16 or wider, within the bound.
No kernel may reach another device: no remote copies, remote signals or barrier semaphores. Data moves between devices by JAX's collectives and lax.ppermute only.
A program may use at most 64 MiB of HBM per device.

```python
import math
import jax
import jax.numpy as jnp
import numpy as np
from jax import lax

D_VIS = 1152
D = 4608
HEAD_DIM = 128
KV_HEADS = 8
Q_HEADS = 16
PAGE = 128
IMAGE_PAGES = 32
IMG_GRP = 2
REQ_GRP = 4
KVW = 1024
QW = 2048
PAGES_DEV = 4
ROWS_DEV = 512
PATCHES = 32768
CAP = 2
RECV = 32
SLOTS_GRP = 256
TOK_GRP = 32256
MAX_LEN = 31872
REQUESTS = 16
N_SECTION = 4
N_KV = 16


def draw_w_proj(key, part):
    column = jnp.arange(D, dtype=jnp.float32) / D
    spread_key = jax.random.fold_in(key, 11)
    entry_key = jax.random.fold_in(key, 12)
    spread = jax.random.uniform(spread_key, (D,), jnp.float32)
    entries = jax.random.normal(entry_key, (D_VIS, D), jnp.float32)
    scales = 10.0 ** (0.5 * column + 0.5 * spread)
    return (entries * scales[None, :] * D_VIS ** (-0.5)).astype(jnp.bfloat16)


def draw_page_owner(key, part):

    def one_group(group_key):
        hottest = jax.random.randint(jax.random.fold_in(group_key, 1), (), 0, N_KV)

        def one_block(block_key):
            shuffled = jax.random.permutation(jax.random.fold_in(block_key, 2), N_KV - 1)
            others = shuffled + (shuffled >= hottest).astype(jnp.int32)
            offset = jax.random.randint(jax.random.fold_in(block_key, 3), (), 0, 2)
            position = jnp.arange(PAGES_DEV, dtype=jnp.int32)
            index = jnp.clip((position - CAP + offset) // CAP, 0, max(N_KV - 2, 0))
            owners = jnp.where(position < CAP, hottest, others[index])
            order = jax.random.permutation(jax.random.fold_in(block_key, 4), PAGES_DEV)
            return owners[order]
        block_keys = jax.random.split(jax.random.fold_in(group_key, 5), N_KV)
        return jax.vmap(one_block)(block_keys).reshape(-1)
    group_keys = jax.random.split(jax.random.fold_in(key, 21), N_SECTION)
    return jax.vmap(one_group)(group_keys).astype(jnp.int32)


def plant(result, rng, least, largest):
    spot = [jax.random.randint(jax.random.fold_in(rng, axis), (), 0, length) for axis, length in enumerate(result.shape)]
    longest = result.shape.index(max(result.shape))
    next_to = spot[:longest] + [(spot[longest] + 1) % result.shape[longest]] + spot[longest + 1:]
    return result.at[tuple(spot)].set(least).at[tuple(next_to)].set(largest)


def shard_levels(rng, dims, shards, low, largest):
    def one(dim, parts):
        steps = jax.random.uniform(jax.random.fold_in(jax.random.fold_in(rng, 6), dim), (parts,), jnp.float32, low / len(shards), largest / len(shards))
        return jnp.repeat(jnp.exp(steps), dims[dim] // parts).reshape((-1,) + (1,) * (len(dims) - dim - 1))

    level = one(*shards[0])
    for cut in shards[1:]:
        level = level * one(*cut)
    return level


def profile(number_of, total, limit, lean):
    portions = [(1 << 20) // math.isqrt(grade ** lean) + 1 for grade in range(2, number_of + 1)]
    spare, counts = total - limit - (number_of - 1), [1] * (number_of - 1)
    while spare > 0:
        free = [i for i in range(number_of - 1) if counts[i] < limit]
        mass, left = sum([portions[i] for i in free]), spare
        for i in free:
            addition = min(limit - counts[i], max(1, left * portions[i] // mass), spare)
            counts[i] = counts[i] + addition
            spare = spare - addition
    return np.array([limit] + counts)


def ragged_sizes(rng, number_of, total, reach, skew):
    if number_of == 2:
        one = jax.random.randint(rng, (), max(1, total - reach), min(reach, total - 1) + 1)
        return jnp.stack([one, total - one])
    tallies = jnp.asarray(profile(number_of, total, reach, skew), jnp.int32)
    twos = (number_of - 1) // 2
    source_of, receiver = tallies[1:1 + 2 * twos:2], tallies[2:2 + 2 * twos:2]
    room = jnp.minimum(source_of - 1, reach - receiver)
    moved = jax.random.randint(jax.random.fold_in(rng, 1), (twos,), 0, 1 << 20) % (room + 1)
    tallies = tallies.at[1:1 + 2 * twos:2].set(source_of - moved).at[2:2 + 2 * twos:2].set(receiver + moved)
    return tallies[jax.random.permutation(jax.random.fold_in(rng, 2), number_of)]


def scatter_about(stream_key, dims, width, reach, cuts=(), held_as=jnp.bfloat16):
    factor_of = shard_levels(stream_key, dims, cuts, -0.22, 0.18) if cuts else 1.0
    drawn = jax.random.normal(stream_key, dims, jnp.float32) * width * factor_of
    return jnp.minimum(jnp.maximum(drawn, -reach), reach).astype(held_as)


def setup_inputs(seed: int = 0) -> dict:
    streams_of = jax.random.split(jax.random.key(seed), 14)
    patches = scatter_about(streams_of[0], (PATCHES, D_VIS), 1.0, 6.0, ((0, 64), (1, 4)))
    vis_gain = jnp.clip(1.0 + 0.18 * jax.random.normal(streams_of[1], (D_VIS,), jnp.float32), 0.1, 1.9)
    vis_bias = scatter_about(streams_of[2], (D_VIS,), 0.5, 3.0, (), jnp.float32)
    w_proj = draw_w_proj(jax.random.fold_in(streams_of[13], 71), 0)
    b_proj = scatter_about(streams_of[4], (D,), 2.0, 12.0, ((0, 4),), jnp.float32)
    rms_gain = jnp.clip(1.0 + 0.18 * jax.random.normal(streams_of[5], (D,), jnp.float32), 0.1, 1.9)
    w_kv = scatter_about(streams_of[6], (D, 2, KVW), D ** -0.5, 0.09375, ((0, 4),))
    queries = scatter_about(streams_of[7], (REQUESTS, QW), 3.0, 18.0, ((0, 4), (1, 4)))
    cache = scatter_about(streams_of[8], (N_SECTION * SLOTS_GRP, PAGE, 2, KVW), 1.0, 6.0, ((0, 64), (3, 4)))
    cache_lengths = jax.vmap(lambda own: ragged_sizes(own, REQ_GRP, TOK_GRP, MAX_LEN, 2))(jax.random.split(streams_of[9], N_SECTION)).reshape((N_SECTION, REQ_GRP)).astype(jnp.int32)
    slot_page = jax.vmap(lambda own: jax.random.permutation(own, SLOTS_GRP))(jax.random.split(streams_of[10], N_SECTION)).reshape((N_SECTION, SLOTS_GRP)).astype(jnp.int32)
    page_owner = draw_page_owner(jax.random.fold_in(streams_of[13], 71), 0)
    image_request = plant(jax.random.randint(streams_of[12], (N_SECTION, IMG_GRP), 0, REQ_GRP), jax.random.fold_in(streams_of[12], 1), 0, REQ_GRP - 1).astype(jnp.int32)
    return dict(patches=patches, vis_gain=vis_gain, vis_bias=vis_bias, w_proj=w_proj, b_proj=b_proj, rms_gain=rms_gain, w_kv=w_kv, queries=queries, cache=cache, cache_lengths=cache_lengths, slot_page=slot_page, page_owner=page_owner, image_request=image_request)


query_scale = 1.0 / 12.0
softcap = 50.0
epsilon = 1e-06

def block_ranks(owners):
    per_block = owners.shape[1]
    same_owner = owners[:, :, None] == owners[:, None, :]
    earlier = jnp.arange(per_block)[None, :] < jnp.arange(per_block)[:, None]
    return lax.optimization_barrier(jnp.sum((same_owner & earlier[None, :, :]).astype(jnp.int32), axis=2))

def encode_group(patch_rows, vis_gain, vis_bias, w_proj, b_proj, rms_gain, w_flat):
    values_in = patch_rows.astype(jnp.float32)
    row_mean = lax.optimization_barrier(jnp.mean(values_in, axis=1, keepdims=True))
    centred = values_in - row_mean
    variance = lax.optimization_barrier(jnp.mean(centred * centred, axis=1, keepdims=True))
    x_norm = (centred * lax.rsqrt(variance + epsilon) * vis_gain + vis_bias).astype(jnp.bfloat16)
    projected = jnp.dot(x_norm, w_proj, preferred_element_type=jnp.float32) + b_proj
    mean_square = lax.optimization_barrier(jnp.mean(projected * projected, axis=1, keepdims=True))
    hidden = (projected * lax.rsqrt(mean_square + epsilon) * rms_gain).astype(jnp.bfloat16)
    return jnp.dot(hidden, w_flat, preferred_element_type=jnp.float32).astype(jnp.bfloat16)

def place_group(pages_group, owners_row):
    owners = owners_row.reshape(N_KV, PAGES_DEV).astype(jnp.int32)
    ranks_grid = block_ranks(owners)
    source = jnp.arange(N_KV, dtype=jnp.int32)[:, None]
    destination = (owners * RECV + source * CAP + ranks_grid).reshape(-1).astype(jnp.int32)
    buffer_zero = jnp.zeros((N_KV * RECV, PAGE, 2, KVW), jnp.bfloat16)
    return buffer_zero.at[destination].set(pages_group)

def attend_group(query_rows, cache_rows, lengths, slot_ids, image_pages, request_row):
    query_grid = query_rows.astype(jnp.float32).reshape(REQ_GRP, KV_HEADS, Q_HEADS // KV_HEADS, HEAD_DIM)
    page_counts = (lengths + PAGE - 1) // PAGE
    starts = jnp.cumsum(page_counts) - page_counts
    within = slot_ids[:, None] - starts[None, :]
    inside = (within >= 0) & (within < page_counts[None, :])
    valid = jnp.where(inside, jnp.clip(lengths[None, :] - within * PAGE, 0, PAGE), 0)
    cache_mask = (jnp.arange(PAGE)[None, :, None] < valid[:, None, :]).reshape(SLOTS_GRP * PAGE, REQ_GRP)
    page_image = jnp.arange(N_KV * PAGES_DEV, dtype=jnp.int32) // IMAGE_PAGES
    page_request = request_row[page_image]
    image_mask = jnp.repeat(page_request[:, None] == jnp.arange(REQ_GRP)[None, :], PAGE, axis=0)
    store = jnp.concatenate([cache_rows, image_pages], axis=0)
    allowed = jnp.concatenate([cache_mask, image_mask], axis=0).T
    keys = store[:, :, 0, :].reshape(-1, KV_HEADS, HEAD_DIM).astype(jnp.float32)
    values = store[:, :, 1, :].reshape(-1, KV_HEADS, HEAD_DIM).astype(jnp.float32)
    raw_scores = jnp.einsum('rkgd,tkd->rkgt', query_grid, keys, precision=lax.Precision.HIGHEST)
    capped = softcap * jnp.tanh(raw_scores * query_scale / softcap)
    weights = jnp.where(allowed[:, None, None, :], jnp.exp(capped), jnp.float32(0.0))
    totals = lax.optimization_barrier(jnp.sum(weights, axis=3))
    rounded = lax.optimization_barrier(weights.astype(jnp.bfloat16)).astype(jnp.float32)
    weighted = jnp.einsum('rkgt,tkd->rkgd', rounded, values, precision=lax.Precision.HIGHEST)
    return (weighted / totals[..., None]).astype(jnp.bfloat16).reshape(REQ_GRP, QW)

def reference(patches, vis_gain, vis_bias, w_proj, b_proj, rms_gain, w_kv, queries, cache, cache_lengths, slot_page, page_owner, image_request):
    w_flat = w_kv.reshape(D, 2 * KVW)
    patch_groups = patches.reshape(N_SECTION, N_KV * ROWS_DEV, D_VIS)
    encoded = lax.map(lambda rows_in: encode_group(rows_in, vis_gain, vis_bias, w_proj, b_proj, rms_gain, w_flat), patch_groups)
    pages_all = encoded.reshape(N_SECTION, N_KV * PAGES_DEV, PAGE, 2, KVW)
    handed = jnp.roll(pages_all, 1, axis=0)
    placed = lax.map(lambda paired: place_group(paired[0], paired[1]), (handed, page_owner))
    new_pages = placed.reshape(N_SECTION * N_KV * RECV, PAGE, 2, KVW)
    group_inputs = (queries.reshape(N_SECTION, REQ_GRP, QW), cache.reshape(N_SECTION, SLOTS_GRP, PAGE, 2, KVW), cache_lengths, slot_page, handed, image_request)
    attended = lax.map(lambda group_in: attend_group(*group_in), group_inputs).reshape(REQUESTS, QW)
    return (new_pages, attended)
```

```python
import functools

import jax
import jax.numpy as jnp
from jax import lax
from jax.experimental import pallas as pl
from jax.experimental.pallas import tpu as pltpu
from jax.sharding import Mesh, PartitionSpec as P

HEAD_DIM = 128
IMAGE_PAGES = 32
PAGE = 128

query_scale = 1.0 / 12.0
softcap = 50.0
epsilon = 1e-06


def block_ranks(owners):
    per_block = owners.shape[1]
    same_owner = owners[:, :, None] == owners[:, None, :]
    earlier = jnp.arange(per_block)[None, :] < jnp.arange(per_block)[:, None]
    return jnp.sum((same_owner & earlier[None, :, :]).astype(jnp.int32), axis=2)


def attend_part(query_grid, keys, values, allowed):
    raw_scores = jnp.einsum("rkgd,tkd->rkgt", query_grid, keys, preferred_element_type=jnp.float32)
    capped = softcap * jnp.tanh(raw_scores * query_scale / softcap)
    weights = jnp.where(allowed[:, None, None, :], jnp.exp(capped), jnp.float32(0.0))
    totals = jnp.sum(weights, axis=3)
    weighted = jnp.einsum(
        "rkgt,tkd->rkgd", weights.astype(jnp.bfloat16), values, preferred_element_type=jnp.float32
    )
    return (totals, weighted)


def encode_kernel(order, x_own, x_left, x_right, x_far, w_own, w_core, w_half, w_both,
                  gain, bias, b_proj, rms_gain, w_kv, out, squares, xs, ws, sems):
    rows = x_own.shape[0]
    copies = []
    for i, ref in enumerate((x_own, x_left, x_right, x_far)):
        copies.append(pltpu.make_async_copy(ref, xs.at[order[i]], sems.at[i]))
    for i, ref in enumerate((w_own, w_core, w_half, w_both)):
        copies.append(pltpu.make_async_copy(ref, ws.at[order[4 + i]], sems.at[4 + i]))
    for c in copies:
        c.start()
    for c in copies:
        c.wait()
    step = 128
    width = 4 * xs.shape[2]

    def body(i, carry):
        at = pl.ds(pl.multiple_of(i * step, step), step)
        parts = [xs[j, at, :].astype(jnp.float32) for j in range(4)]
        mean = sum(jnp.sum(p, axis=1, keepdims=True) for p in parts) / width
        parts = [p - mean for p in parts]
        var = sum(jnp.sum(p * p, axis=1, keepdims=True) for p in parts) / width
        inv = lax.rsqrt(var + epsilon)
        acc = None
        for j in range(4):
            xn = (parts[j] * inv * gain[j] + bias[j]).astype(jnp.bfloat16)
            d = jnp.dot(xn, ws[j], preferred_element_type=jnp.float32)
            acc = d if acc is None else acc + d
        projected = acc + b_proj[...]
        sq = jnp.sum(projected * projected, axis=1, keepdims=True)
        squares[:, at] = jnp.transpose(jnp.broadcast_to(sq, (step, 128)))[:8]
        hidden = (projected * rms_gain[...]).astype(jnp.bfloat16)
        res = jnp.dot(hidden, w_kv[...], preferred_element_type=jnp.float32).astype(jnp.bfloat16)
        for t in range(4):
            out[t, at, 0:256] = res[:, t * 256 : (t + 1) * 256]
            out[t, at, 256:512] = res[:, 1024 + t * 256 : 1024 + (t + 1) * 256]
        return carry

    lax.fori_loop(0, rows // step, body, 0)


def encode(order, xs, ws, gain, bias, b_proj, rms_gain, w_kv):
    rows = xs[0].shape[0]
    any_spec = pl.BlockSpec(memory_space=pl.ANY)
    vmem = pl.BlockSpec(memory_space=pltpu.VMEM)
    return pl.pallas_call(
        encode_kernel,
        out_shape=(
            jax.ShapeDtypeStruct((4, rows, 512), jnp.bfloat16),
            jax.ShapeDtypeStruct((8, rows), jnp.float32),
        ),
        in_specs=[pl.BlockSpec(memory_space=pltpu.SMEM)] + [any_spec] * 8 + [vmem] * 5,
        out_specs=(vmem, vmem),
        scratch_shapes=[
            pltpu.VMEM((4, rows, 288), jnp.bfloat16),
            pltpu.VMEM((4, 288, 1152), jnp.bfloat16),
            pltpu.SemaphoreType.DMA((8,)),
        ],
        compiler_params=pltpu.CompilerParams(vmem_limit_bytes=40 << 20),
        name="encode",
    )(order, *xs, *ws, gain, bias, b_proj, rms_gain, w_kv)


def pick_kernel(code, first, second, zero, out, sem):
    for i in range(8):
        c = code[i]

        @pl.when(c < 0)
        def _():
            pltpu.make_async_copy(zero, out.at[i], sem).start()

        @pl.when((c >= 0) & (c < 4))
        def _():
            pltpu.make_async_copy(first.at[c], out.at[i], sem).start()

        @pl.when(c >= 4)
        def _():
            pltpu.make_async_copy(second.at[c - 4], out.at[i], sem).start()

    for i in range(8):
        pltpu.make_async_copy(zero, out.at[i], sem).wait()


def pick(code, first, second, zero):
    any_spec = pl.BlockSpec(memory_space=pl.ANY)
    return pl.pallas_call(
        pick_kernel,
        out_shape=jax.ShapeDtypeStruct((8,) + first.shape[1:], first.dtype),
        in_specs=[pl.BlockSpec(memory_space=pltpu.SMEM), any_spec, any_spec, any_spec],
        out_specs=any_spec,
        scratch_shapes=[pltpu.SemaphoreType.DMA],
        name="pick",
    )(code, first, second, zero)


def per_device(
    patches, vis_gain, vis_bias, w_proj, b_proj, rms_gain, w_kv, queries, cache,
    cache_lengths, slot_page, page_owner, image_request,
):
    zh, co, zl = lax.axis_index("zh"), lax.axis_index("co"), lax.axis_index("zl")
    y, tp = lax.axis_index("y"), lax.axis_index("tp")
    section = zh * 2 + co

    hop = []
    for a in range(2):
        for z in range(4):
            hop.append((a * 8 + z, a * 8 + 4 + z))
            hop.append((a * 8 + 4 + z, (1 - a) * 8 + (z ^ 2)))
    x_own = lax.ppermute(patches, ("zh", "co", "zl"), hop)

    swap = [(0, 1), (1, 0)]
    w_core = lax.ppermute(w_proj, "co", swap)
    piece_rows = w_proj.shape[0] // 4
    piece = lax.dynamic_slice_in_dim(w_proj, y * piece_rows, piece_rows, 0)
    cross = [(a * 4 + z, (1 - a) * 4 + (z ^ 2)) for a in range(2) for z in range(4)]
    piece = lax.ppermute(piece, ("zh", "zl"), cross)
    ring = lambda n: [(i, (i + n) % 4) for i in range(4)]
    p1 = lax.ppermute(piece, "y", ring(1))
    p3 = lax.ppermute(piece, "y", ring(3))
    p2 = lax.ppermute(piece, "y", ring(2))
    w_half = jnp.zeros((4,) + piece.shape, piece.dtype)
    for k, p in ((0, piece), (1, p1), (2, p2), (3, p3)):
        w_half = lax.dynamic_update_index_in_dim(w_half, p, (y - k) % 4, 0)
    w_half = w_half.reshape(w_proj.shape)
    w_both = lax.ppermute(w_half, "co", swap)

    half = x_own.shape[0] // 2
    x_left = lax.ppermute(x_own, "tp", ring(1))
    x_right = lax.ppermute(x_own, "tp", ring(3))
    far_a = lax.ppermute(x_left[:half], "tp", ring(1))
    far_b = lax.ppermute(x_right[half:], "tp", ring(3))
    x_far = jnp.concatenate([far_a, far_b], axis=0)

    order = jnp.stack(
        [tp, (tp + 3) % 4, (tp + 1) % 4, (tp + 2) % 4, section, section ^ 1, section ^ 2, section ^ 3]
    ).astype(jnp.int32)
    w_kv2 = w_kv.reshape(w_kv.shape[0], -1)
    partial, squares = encode(
        order, (x_own, x_left, x_right, x_far), (w_proj, w_core, w_half, w_both),
        vis_gain.reshape(4, 1, 288), vis_bias.reshape(4, 1, 288),
        b_proj.reshape(1, -1), rms_gain.reshape(1, -1), w_kv2,
    )
    total_sq = squares
    for n in (1, 3, 2):
        total_sq = total_sq + lax.ppermute(squares, "tp", ring(n))
    scale = lax.rsqrt(total_sq[0] / (b_proj.shape[0] * 4) + epsilon)
    parts = lax.all_to_all(partial, "tp", 0, 0, tiled=True)
    summed = jnp.sum(parts.astype(jnp.float32), axis=0)
    image_kv = (summed * scale[:, None]).astype(jnp.bfloat16)
    pages = jnp.stack(
        [image_kv[:, :256].reshape(4, PAGE, 256), image_kv[:, 256:].reshape(4, PAGE, 256)], axis=2
    )

    owners = lax.dynamic_index_in_dim(page_owner, section, 0, keepdims=False).reshape(16, 4)
    ranks = block_ranks(owners)
    flip = jnp.where(co == 0, 2, 0)
    first3 = jnp.stack([zl, zl ^ 1, jnp.where(zl < 2, 2, 1), jnp.where(zl < 2, 3, 0)])
    z_src = first3 ^ flip
    k_src = z_src * 4 + y
    own_rows = owners[k_src]
    rank_rows = ranks[k_src]
    want_owner = (zl * 4 + jnp.arange(8) // 2)[None, :, None]
    want_rank = (jnp.arange(8) % 2)[None, :, None]
    match = (own_rows[:, None, :] == want_owner) & (rank_rows[:, None, :] == want_rank)
    code = jnp.sum(jnp.where(match, jnp.arange(4)[None, None, :] + 1, 0), axis=2) - 1
    middle = (zl == 1) | (zl == 2)
    shift = jnp.where(middle, 0, 4) * jnp.array([0, 0, 1, 1])
    code = jnp.where(code >= 0, code + shift[:, None], -1).astype(jnp.int32)

    zero = jnp.zeros((PAGE, 2, 256), jnp.bfloat16)
    pair = [(0, 1), (1, 0), (2, 3), (3, 2)]
    mid = [(1, 2), (2, 1)]
    outer = [(1, 0), (2, 3)]
    b1 = lax.ppermute(pages, "zl", pair)
    b2m = lax.ppermute(pages, "zl", mid)
    b3m = lax.ppermute(b1, "zl", mid)
    b2o = lax.ppermute(b2m, "zl", outer)
    b3o = lax.ppermute(b3m, "zl", outer)
    new_pages = jnp.zeros((32, PAGE, 2, 256), jnp.bfloat16)
    for i, (f, s) in enumerate(((pages, pages), (b1, b1), (b2m, b2o), (b3m, b3o))):
        sent = pick(code[i], f, s, zero)
        got = lax.all_to_all(sent, "y", 0, 0, tiled=True)
        new_pages = lax.dynamic_update_slice_in_dim(new_pages, got, z_src[i] * 8, 0)

    req_count = queries.shape[0]
    query_grid = queries.reshape(req_count, 2, 2, HEAD_DIM)
    lengths = cache_lengths[0]
    page_counts = (lengths + PAGE - 1) // PAGE
    starts = jnp.cumsum(page_counts) - page_counts
    within = slot_page[0][:, None] - starts[None, :]
    inside = (within >= 0) & (within < page_counts[None, :])
    valid = jnp.where(inside, jnp.clip(lengths[None, :] - within * PAGE, 0, PAGE), 0)
    cache_mask = jnp.arange(PAGE)[None, :, None] < valid[:, None, :]
    keys = cache[:, :, 0, :].reshape(-1, 2, HEAD_DIM)
    values = cache[:, :, 1, :].reshape(-1, 2, HEAD_DIM)
    c_tot, c_num = attend_part(query_grid, keys, values, cache_mask.reshape(-1, req_count).T)
    my_request = lax.dynamic_index_in_dim(image_request[0], (zl ^ flip) // 2, 0, keepdims=False)
    i_mask = jnp.broadcast_to((jnp.arange(req_count) == my_request)[:, None], (req_count, image_kv.shape[0]))
    i_tot, i_num = attend_part(
        query_grid, image_kv[:, :256].reshape(-1, 2, HEAD_DIM), image_kv[:, 256:].reshape(-1, 2, HEAD_DIM), i_mask
    )
    tot = (c_tot + i_tot).reshape(16)
    num = (c_num + i_num).reshape(16, HEAD_DIM)
    both = jnp.concatenate([num, jnp.broadcast_to(tot[:, None], num.shape)], axis=0)
    for axis in ("y", "zl"):
        for m in (1, 2):
            both = both + lax.ppermute(both, axis, [(i, i ^ m) for i in range(4)])
    attended = (both[:16] / both[16:]).astype(jnp.bfloat16).reshape(req_count, -1)
    return (new_pages, attended)


def solution(mesh):
    fine = Mesh(mesh.devices.reshape(2, 2, 4, 4, 4), ("zh", "co", "zl", "y", "tp"))
    sec, kv, every = ("zh", "co"), ("zl", "y"), ("zh", "co", "zl", "y")
    in_specs = (
        P(every, "tp"), P(), P(), P(sec, "tp"), P("tp"), P("tp"), P("tp", None, None), P(sec, "tp"),
        P(every, None, None, "tp"), P(sec, None), P(sec, kv), P(), P(sec, None),
    )
    out_specs = (P(every, None, None, "tp"), P(sec, "tp"))
    return jax.shard_map(per_device, mesh=fine, in_specs=in_specs, out_specs=out_specs, check_vma=False)
```

```python
import functools

import jax
import jax.numpy as jnp
from jax import lax
from jax.experimental import pallas as pl
from jax.experimental.pallas import tpu as pltpu
from jax.sharding import Mesh, PartitionSpec as P

HEAD_DIM = 128
IMAGE_PAGES = 32
PAGE = 128

query_scale = 1.0 / 12.0
softcap = 50.0
epsilon = 1e-06


def block_ranks(owners):
    per_block = owners.shape[1]
    same_owner = owners[:, :, None] == owners[:, None, :]
    earlier = jnp.arange(per_block)[None, :] < jnp.arange(per_block)[:, None]
    return jnp.sum((same_owner & earlier[None, :, :]).astype(jnp.int32), axis=2)


def attend_part(query_grid, keys, values, allowed):
    raw_scores = jnp.einsum("rkgd,tkd->rkgt", query_grid, keys, preferred_element_type=jnp.float32)
    capped = softcap * jnp.tanh(raw_scores * query_scale / softcap)
    weights = jnp.where(allowed[:, None, None, :], jnp.exp(capped), jnp.float32(0.0))
    totals = jnp.sum(weights, axis=3)
    weighted = jnp.einsum(
        "rkgt,tkd->rkgd", weights.astype(jnp.bfloat16), values, preferred_element_type=jnp.float32
    )
    return (totals, weighted)


def encode_kernel(order, x_own, x_left, x_right, x_far, w_own, w_core, w_half, w_both,
                  gain, bias, b_proj, rms_gain, w_kv, out, squares, xs, ws, sems):
    rows = x_own.shape[0]
    copies = []
    for i, ref in enumerate((x_own, x_left, x_right, x_far)):
        copies.append(pltpu.make_async_copy(ref, xs.at[order[i]], sems.at[i]))
    for i, ref in enumerate((w_own, w_core, w_half, w_both)):
        copies.append(pltpu.make_async_copy(ref, ws.at[order[4 + i]], sems.at[4 + i]))
    for c in copies:
        c.start()
    for c in copies:
        c.wait()
    step = 128
    width = 4 * xs.shape[2]

    def body(i, carry):
        at = pl.ds(pl.multiple_of(i * step, step), step)
        parts = [xs[j, at, :].astype(jnp.float32) for j in range(4)]
        mean = sum(jnp.sum(p, axis=1, keepdims=True) for p in parts) / width
        parts = [p - mean for p in parts]
        var = sum(jnp.sum(p * p, axis=1, keepdims=True) for p in parts) / width
        inv = lax.rsqrt(var + epsilon)
        acc = None
        for j in range(4):
            xn = (parts[j] * inv * gain[j] + bias[j]).astype(jnp.bfloat16)
            d = jnp.dot(xn, ws[j], preferred_element_type=jnp.float32)
            acc = d if acc is None else acc + d
        projected = acc + b_proj[...]
        sq = jnp.sum(projected * projected, axis=1, keepdims=True)
        squares[:, at] = jnp.transpose(jnp.broadcast_to(sq, (step, 128)))[:8]
        hidden = (projected * rms_gain[...]).astype(jnp.bfloat16)
        res = jnp.dot(hidden, w_kv[...], preferred_element_type=jnp.float32).astype(jnp.bfloat16)
        for t in range(4):
            out[t, at, 0:256] = res[:, t * 256 : (t + 1) * 256]
            out[t, at, 256:512] = res[:, 1024 + t * 256 : 1024 + (t + 1) * 256]
        return carry

    lax.fori_loop(0, rows // step, body, 0)


def encode(order, xs, ws, gain, bias, b_proj, rms_gain, w_kv):
    rows = xs[0].shape[0]
    any_spec = pl.BlockSpec(memory_space=pl.ANY)
    vmem = pl.BlockSpec(memory_space=pltpu.VMEM)
    return pl.pallas_call(
        encode_kernel,
        out_shape=(
            jax.ShapeDtypeStruct((4, rows, 512), jnp.bfloat16),
            jax.ShapeDtypeStruct((8, rows), jnp.float32),
        ),
        in_specs=[pl.BlockSpec(memory_space=pltpu.SMEM)] + [any_spec] * 8 + [vmem] * 5,
        out_specs=(vmem, vmem),
        scratch_shapes=[
            pltpu.VMEM((4, rows, 288), jnp.bfloat16),
            pltpu.VMEM((4, 288, 1152), jnp.bfloat16),
            pltpu.SemaphoreType.DMA((8,)),
        ],
        compiler_params=pltpu.CompilerParams(vmem_limit_bytes=40 << 20),
        name="encode",
    )(order, *xs, *ws, gain, bias, b_proj, rms_gain, w_kv)


def pick_kernel(code, first, second, zero, out, sem):
    for i in range(8):
        c = code[i]

        @pl.when(c < 0)
        def _():
            pltpu.make_async_copy(zero, out.at[i], sem).start()

        @pl.when((c >= 0) & (c < 4))
        def _():
            pltpu.make_async_copy(first.at[c], out.at[i], sem).start()

        @pl.when(c >= 4)
        def _():
            pltpu.make_async_copy(second.at[c - 4], out.at[i], sem).start()

    for i in range(8):
        pltpu.make_async_copy(zero, out.at[i], sem).wait()


def pick(code, first, second, zero):
    vmem = pl.BlockSpec(memory_space=pltpu.VMEM)
    return pl.pallas_call(
        pick_kernel,
        out_shape=jax.ShapeDtypeStruct((8,) + first.shape[1:], first.dtype),
        in_specs=[pl.BlockSpec(memory_space=pltpu.SMEM), vmem, vmem, vmem],
        out_specs=pl.BlockSpec(memory_space=pl.ANY),
        scratch_shapes=[pltpu.SemaphoreType.DMA],
        name="pick",
    )(code, first, second, zero)


def place_kernel(where, got, *refs):
    out, sem = refs[-2:]
    copy = pltpu.make_async_copy(got, out.at[pl.ds(where[0] * 8, 8)], sem)
    copy.start()
    copy.wait()


def place(where, got, buffer):
    any_spec = pl.BlockSpec(memory_space=pl.ANY)
    vmem = pl.BlockSpec(memory_space=pltpu.VMEM)
    given = (where, got) if buffer is None else (where, got, buffer)
    return pl.pallas_call(
        place_kernel,
        out_shape=jax.ShapeDtypeStruct((32,) + got.shape[1:], got.dtype),
        in_specs=[pl.BlockSpec(memory_space=pltpu.SMEM), vmem] + [any_spec] * (len(given) - 2),
        out_specs=any_spec,
        scratch_shapes=[pltpu.SemaphoreType.DMA],
        input_output_aliases={} if buffer is None else {2: 0},
        name="place",
    )(*given)


def per_device(
    patches, vis_gain, vis_bias, w_proj, b_proj, rms_gain, w_kv, queries, cache,
    cache_lengths, slot_page, page_owner, image_request,
):
    zh, co, zl = lax.axis_index("zh"), lax.axis_index("co"), lax.axis_index("zl")
    y, tp = lax.axis_index("y"), lax.axis_index("tp")
    section = zh * 2 + co

    hop = []
    for a in range(2):
        for z in range(4):
            hop.append((a * 8 + z, a * 8 + 4 + z))
            hop.append((a * 8 + 4 + z, (1 - a) * 8 + (z ^ 2)))
    x_own = lax.ppermute(patches, ("zh", "co", "zl"), hop)

    swap = [(0, 1), (1, 0)]
    w_core = lax.ppermute(w_proj, "co", swap)
    piece_rows = w_proj.shape[0] // 4
    piece = lax.dynamic_slice_in_dim(w_proj, y * piece_rows, piece_rows, 0)
    cross = [(a * 4 + z, (1 - a) * 4 + (z ^ 2)) for a in range(2) for z in range(4)]
    piece = lax.ppermute(piece, ("zh", "zl"), cross)
    ring = lambda n: [(i, (i + n) % 4) for i in range(4)]
    p1 = lax.ppermute(piece, "y", ring(1))
    p3 = lax.ppermute(piece, "y", ring(3))
    p2 = lax.ppermute(piece, "y", ring(2))
    w_half = jnp.zeros((4,) + piece.shape, piece.dtype)
    for k, p in ((0, piece), (1, p1), (2, p2), (3, p3)):
        w_half = lax.dynamic_update_index_in_dim(w_half, p, (y - k) % 4, 0)
    w_half = w_half.reshape(w_proj.shape)
    w_both = lax.ppermute(w_half, "co", swap)

    half = x_own.shape[0] // 2
    x_left = lax.ppermute(x_own, "tp", ring(1))
    x_right = lax.ppermute(x_own, "tp", ring(3))
    far_a = lax.ppermute(x_left[:half], "tp", ring(1))
    far_b = lax.ppermute(x_right[half:], "tp", ring(3))
    x_far = jnp.concatenate([far_a, far_b], axis=0)

    order = jnp.stack(
        [tp, (tp + 3) % 4, (tp + 1) % 4, (tp + 2) % 4, section, section ^ 1, section ^ 2, section ^ 3]
    ).astype(jnp.int32)
    w_kv2 = w_kv.reshape(w_kv.shape[0], -1)
    partial, squares = encode(
        order, (x_own, x_left, x_right, x_far), (w_proj, w_core, w_half, w_both),
        vis_gain.reshape(4, 1, 288), vis_bias.reshape(4, 1, 288),
        b_proj.reshape(1, -1), rms_gain.reshape(1, -1), w_kv2,
    )
    total_sq = squares
    for n in (1, 3, 2):
        total_sq = total_sq + lax.ppermute(squares, "tp", ring(n))
    scale = lax.rsqrt(total_sq[0] / (b_proj.shape[0] * 4) + epsilon)
    parts = lax.all_to_all(partial, "tp", 0, 0, tiled=True)
    summed = jnp.sum(parts.astype(jnp.float32), axis=0)
    image_kv = (summed * scale[:, None]).astype(jnp.bfloat16)
    pages = jnp.stack(
        [image_kv[:, :256].reshape(4, PAGE, 256), image_kv[:, 256:].reshape(4, PAGE, 256)], axis=2
    )

    owners = lax.dynamic_index_in_dim(page_owner, section, 0, keepdims=False).reshape(16, 4)
    ranks = block_ranks(owners)
    flip = jnp.where(co == 0, 2, 0)
    first3 = jnp.stack([zl, zl ^ 1, jnp.where(zl < 2, 2, 1), jnp.where(zl < 2, 3, 0)])
    z_src = first3 ^ flip
    k_src = z_src * 4 + y
    own_rows = owners[k_src]
    rank_rows = ranks[k_src]
    want_owner = (zl * 4 + jnp.arange(8) // 2)[None, :, None]
    want_rank = (jnp.arange(8) % 2)[None, :, None]
    match = (own_rows[:, None, :] == want_owner) & (rank_rows[:, None, :] == want_rank)
    code = jnp.sum(jnp.where(match, jnp.arange(4)[None, None, :] + 1, 0), axis=2) - 1
    middle = (zl == 1) | (zl == 2)
    shift = jnp.where(middle, 0, 4) * jnp.array([0, 0, 1, 1])
    code = jnp.where(code >= 0, code + shift[:, None], -1).astype(jnp.int32)

    zero = jnp.zeros((PAGE, 2, 256), jnp.bfloat16)
    pair = [(0, 1), (1, 0), (2, 3), (3, 2)]
    mid = [(1, 2), (2, 1)]
    outer = [(1, 0), (2, 3)]
    b1 = lax.ppermute(pages, "zl", pair)
    b2m = lax.ppermute(pages, "zl", mid)
    b3m = lax.ppermute(b1, "zl", mid)
    b2o = lax.ppermute(b2m, "zl", outer)
    b3o = lax.ppermute(b3m, "zl", outer)
    new_pages = None
    for i, (f, s) in enumerate(((pages, pages), (b1, b1), (b2m, b2o), (b3m, b3o))):
        sent = pick(code[i], f, s, zero)
        got = lax.all_to_all(sent, "y", 0, 0, tiled=True)
        new_pages = place(z_src[i : i + 1].astype(jnp.int32), got, new_pages)

    req_count = queries.shape[0]
    query_grid = queries.reshape(req_count, 2, 2, HEAD_DIM)
    lengths = cache_lengths[0]
    page_counts = (lengths + PAGE - 1) // PAGE
    starts = jnp.cumsum(page_counts) - page_counts
    within = slot_page[0][:, None] - starts[None, :]
    inside = (within >= 0) & (within < page_counts[None, :])
    valid = jnp.where(inside, jnp.clip(lengths[None, :] - within * PAGE, 0, PAGE), 0)
    cache_mask = jnp.arange(PAGE)[None, :, None] < valid[:, None, :]
    keys = cache[:, :, 0, :].reshape(-1, 2, HEAD_DIM)
    values = cache[:, :, 1, :].reshape(-1, 2, HEAD_DIM)
    c_tot, c_num = attend_part(query_grid, keys, values, cache_mask.reshape(-1, req_count).T)
    my_request = lax.dynamic_index_in_dim(image_request[0], (zl ^ flip) // 2, 0, keepdims=False)
    i_mask = jnp.broadcast_to((jnp.arange(req_count) == my_request)[:, None], (req_count, image_kv.shape[0]))
    i_tot, i_num = attend_part(
        query_grid, image_kv[:, :256].reshape(-1, 2, HEAD_DIM), image_kv[:, 256:].reshape(-1, 2, HEAD_DIM), i_mask
    )
    tot = (c_tot + i_tot).reshape(16)
    num = (c_num + i_num).reshape(16, HEAD_DIM)
    both = jnp.concatenate([num, jnp.broadcast_to(tot[:, None], num.shape)], axis=0)
    for axis in ("y", "zl"):
        for m in (1, 2):
            both = both + lax.ppermute(both, axis, [(i, i ^ m) for i in range(4)])
    attended = (both[:16] / both[16:]).astype(jnp.bfloat16).reshape(req_count, -1)
    return (new_pages, attended)


def solution(mesh):
    fine = Mesh(mesh.devices.reshape(2, 2, 4, 4, 4), ("zh", "co", "zl", "y", "tp"))
    sec, kv, every = ("zh", "co"), ("zl", "y"), ("zh", "co", "zl", "y")
    in_specs = (
        P(every, "tp"), P(), P(), P(sec, "tp"), P("tp"), P("tp"), P("tp", None, None), P(sec, "tp"),
        P(every, None, None, "tp"), P(sec, None), P(sec, kv), P(), P(sec, None),
    )
    out_specs = (P(every, None, None, "tp"), P(sec, "tp"))
    return jax.shard_map(per_device, mesh=fine, in_specs=in_specs, out_specs=out_specs, check_vma=False)
```
